32 devices in a mesh: tm: 2 (over x), vox: 8 (over z, y), feat: 2 (over core).
Axes of the slice: x: 2, y: 2, z: 4, core: 2. Of those that a mesh axis runs over, the one named last changes fastest.
Arguments:
- design_matrix: bfloat16 [256, 4096], P(None, ('tm', 'feat')), may hold values from -6 to 6
- measured_signals: bfloat16 [256, 16384], P('tm', 'vox'), may hold values from -6 to 6
- predictor_group_label: int32 [4096], P('vox'), may hold values from 0 to 3
- shrinkage_weights: float32 [2, 4], replicated, may hold values from 0.1 to 10
- target_shrink_choice: int32 [256], P('vox'), may hold values from 0 to 1
Outputs:
- trailing: float32 [2, 4096, 4096], P(None, ('tm', 'feat'), 'vox')
- right_sides: float32 [4096, 16384], P(('tm', 'feat'), 'vox')
The draws below stay inside these ranges and needn't reach their ends.
All inputs are finite; a program needn't handle non-finite values.
Results may differ from the reference program's by a relative error of at most 0.0003.
Values may be sent and summed in bfloat16 or wider, within the bound.
No kernel may reach another device: no remote copies, remote signals or barrier semaphores. Data moves between devices by JAX's collectives and lax.ppermute only.
A program may use at most 128 MiB of HBM per device.

```python
import math
import jax
import jax.numpy as jnp
from jax import lax

P_SIZE = 4096
V = 16384
PREDICTOR_GROUPS = 4
SHRINK_OPTIONS = 2
GROUP = 64
STEPS = 1
TIME = 256
CB = 512


def plant(values, stream_key, least, top_value):
    extent = values.shape
    index_at = [jax.random.randint(jax.random.fold_in(stream_key, axis), (), 0, extent[axis]) for axis in range(len(extent))]
    values = values.at[tuple(index_at)].set(least)
    longest = extent.index(max(extent))
    index_at[longest] = (index_at[longest] + 1) % extent[longest]
    return values.at[tuple(index_at)].set(top_value)


def block_levels(key, shape, shards, low, largest):
    loudness, own = 1.0, jax.random.fold_in(key, 6)
    for position, parts in shards:
        draws = jnp.exp(jax.random.uniform(jax.random.fold_in(own, position), (parts,), jnp.float32, low / len(shards), largest / len(shards)))
        loudness = loudness * jnp.repeat(draws, shape[position] // parts).reshape([-1 if axis == position else 1 for axis in range(len(shape))])
    return loudness


def bell_draw(stream_key, shape, spread, most, shards=(), held_as=jnp.bfloat16):
    gain = block_levels(stream_key, shape, shards, -0.22, 0.18) if shards else 1.0
    entries = jax.random.normal(stream_key, shape, jnp.float32) * spread * gain
    return jnp.minimum(jnp.maximum(entries, -most), most).astype(held_as)


def setup_inputs(seed: int = 0) -> dict:
    key_list = jax.random.split(jax.random.key(seed), 6)
    return {
        "design_matrix": bell_draw(key_list[0], (TIME, P_SIZE), 1.0, 6.0, ((1, 4),)),
        "measured_signals": bell_draw(key_list[1], (TIME, V), 1.0, 6.0, ((0, 2), (1, 8))),
        "predictor_group_label": plant(jax.random.randint(key_list[2], (P_SIZE,), 0, PREDICTOR_GROUPS), jax.random.fold_in(key_list[2], 1), 0, PREDICTOR_GROUPS - 1).astype(jnp.int32),
        "shrinkage_weights": jnp.clip(jnp.exp(jax.random.uniform(key_list[3], (SHRINK_OPTIONS, PREDICTOR_GROUPS), jnp.float32, math.log(0.1), math.log(10.0))), 0.1, 10.0),
        "target_shrink_choice": plant(jax.random.randint(key_list[4], (V // GROUP,), 0, SHRINK_OPTIONS), jax.random.fold_in(key_list[4], 1), 0, SHRINK_OPTIONS - 1).astype(jnp.int32),
    }


def reference(design_matrix, measured_signals, predictor_group_label, shrinkage_weights, target_shrink_choice):
    gram = jnp.dot(design_matrix.T.astype(jnp.float32), design_matrix.astype(jnp.float32), preferred_element_type=jnp.float32) / TIME
    predictor_shrinkage = shrinkage_weights[:, predictor_group_label]
    system = gram[None, :, :] + jax.vmap(jnp.diag)(predictor_shrinkage)
    sides = jnp.dot(design_matrix.T.astype(jnp.float32), measured_signals.astype(jnp.float32), preferred_element_type=jnp.float32) / math.sqrt(TIME)
    first_ridge = jnp.repeat(target_shrink_choice, GROUP) == 0
    global_rows = jnp.arange(P_SIZE)
    for panel_step in range(STEPS):
        block_start = panel_step * CB
        factor = jnp.linalg.cholesky(system[:, block_start:block_start + CB, block_start:block_start + CB])
        solved = lax.linalg.triangular_solve(factor, system[:, :, block_start:block_start + CB], left_side=False, lower=True, transpose_a=True)
        panel = jnp.where((global_rows >= block_start)[None, :, None], solved, 0.0)
        block_sides = jnp.broadcast_to(sides[block_start:block_start + CB], (SHRINK_OPTIONS, CB, V))
        solutions = lax.linalg.triangular_solve(factor, block_sides, left_side=True, lower=True)
        solved_sides = jnp.where(first_ridge[None, :], solutions[0], solutions[1])
        system = system - jnp.einsum('brk,bck->brc', panel, panel, precision=lax.Precision.HIGHEST)
        update_first = jnp.dot(panel[0], solved_sides, precision=lax.Precision.HIGHEST)
        update_second = jnp.dot(panel[1], solved_sides, precision=lax.Precision.HIGHEST)
        sides = sides - jnp.where(first_ridge[None, :], update_first, update_second)
        sides = sides.at[block_start:block_start + CB].set(solved_sides)
    return (system, sides)
```

```python
import jax
import jax.numpy as jnp
from jax import lax
from jax.experimental import pallas as pl
from jax.experimental.pallas import tpu as pltpu
from jax.sharding import PartitionSpec as P

GROUP = 64
B = 128
F32 = jnp.float32
BF16 = jnp.bfloat16
HI = lax.Precision.HIGHEST
AXES = ("tm", "vox", "feat")
FIRST = (((0,), (0,)), ((), ()))


def lane_b(v, lane):
    return jnp.broadcast_to(v[:, lane : lane + 1], (8, B))


def sub_b(v, row):
    return jnp.broadcast_to(v[row : row + 1, :], (8, B))


def inverse_factors(tiles):
    n = B // 8
    lanes = lax.broadcasted_iota(jnp.int32, (8, B), 1)
    subs = lax.broadcasted_iota(jnp.int32, (8, B), 0)
    strips = [[t[8 * i : 8 * i + 8, :] for i in range(n)] for t in tiles]
    done = [[] for _ in tiles]
    for s in range(n):
        pivot_lanes = (lanes >= 8 * s) & (lanes < 8 * s + 8)
        for r in range(len(tiles)):
            st = strips[r]
            rows = [sub_b(st[s], k) for k in range(8)]
            e = [[lane_b(rows[k], 8 * s + j) if j >= k else None for j in range(8)] for k in range(8)]
            rows = [
                jnp.where(pivot_lanes, jnp.where(lanes == 8 * s + k, 1.0, 0.0), rows[k]) for k in range(8)
            ]
            m = {}
            recips = []
            for j in range(8):
                recip = 1.0 / e[j][j]
                recips.append(recip)
                for k in range(j + 1, 8):
                    m[k, j] = e[j][k] * recip
                    for l in range(k, 8):
                        e[k][l] = e[k][l] - m[k, j] * e[j][l]
                    rows[k] = rows[k] - m[k, j] * rows[j]
            out = jnp.zeros((8, B), F32)
            for k in range(8):
                out = jnp.where(subs == k, rows[k] * lax.rsqrt(e[k][k]), out)
            done[r].append(jnp.where(lanes < 8 * s + 8, out, 0.0))
            if s + 1 < n:
                v = [None] * 8
                for k in range(7, -1, -1):
                    acc = rows[k] * recips[k]
                    for l in range(k + 1, 8):
                        acc = acc - m[l, k] * v[l]
                    v[k] = acc
                for t in range(s + 1, n):
                    cols = [lane_b(st[t], 8 * s + j) for j in range(8)]
                    acc = jnp.where(pivot_lanes, 0.0, st[t])
                    for j in range(8):
                        acc = acc - cols[j] * v[j]
                    st[t] = acc
    return [jnp.concatenate(d, axis=0) for d in done]


def factor_kernel(weights_ref, x_ref, label_ref, w_ref, k_ref, m_ref):
    options, groups = weights_ref.shape
    time, width = x_ref.shape
    nk = width // B
    nm = (width + time) // B
    x = x_ref[...]
    row = lax.broadcasted_iota(jnp.int32, (B, B), 0)
    col = lax.broadcasted_iota(jnp.int32, (B, B), 1)
    eye = lax.broadcasted_iota(jnp.int32, (time, time), 0) == lax.broadcasted_iota(
        jnp.int32, (time, time), 1
    )
    eye = jnp.where(eye, 1.0, 0.0)
    gram = lax.dot_general(x, x, FIRST, preferred_element_type=F32) * (1.0 / time)
    xt = lax.dot_general(x, eye.astype(BF16), FIRST, preferred_element_type=F32) * time**-0.5
    for r in range(options):
        m_ref[r, :width, :width] = gram
        m_ref[r, :width, width:] = xt
        m_ref[r, width:, width:] = eye
        for k in range(nk):
            at = slice(k * B, (k + 1) * B)
            ridge = jnp.zeros((1, B), F32)
            for g in range(groups):
                ridge = jnp.where(label_ref[:, at] == g, weights_ref[r, g], ridge)
            m_ref[r, at, at] = gram[at, at] + jnp.where(row == col, ridge, 0.0)

    def step(k, _):
        at = pl.ds(pl.multiple_of(k * B, B), B)
        inverses = inverse_factors([m_ref[r, at, at] for r in range(options)])
        for r in range(options):
            m_ref[r, at, :] = jnp.dot(inverses[r], m_ref[r, at, :], precision=HI)

        def rest(j, _):
            to = pl.ds(pl.multiple_of(j * B, B), B)
            for r in range(options):
                m_ref[r, to, :] -= lax.dot_general(
                    m_ref[r, at, to], m_ref[r, at, :], FIRST, precision=HI, preferred_element_type=F32
                )
            return 0

        lax.fori_loop(k + 1, nm, rest, 0)
        return 0

    lax.fori_loop(0, nk, step, 0)
    for r in range(options):
        w_ref[r] = m_ref[r, :width, width:]
        k_ref[r] = m_ref[r, width:, width:]


def factor(weights, x, labels):
    time, width = x.shape
    options = weights.shape[0]
    n = time + width
    vmem = pl.BlockSpec(memory_space=pltpu.VMEM)
    return pl.pallas_call(
        factor_kernel,
        out_shape=(
            jax.ShapeDtypeStruct((options, width, time), F32),
            jax.ShapeDtypeStruct((options, time, time), F32),
        ),
        in_specs=[pl.BlockSpec(memory_space=pltpu.SMEM), vmem, vmem],
        out_specs=(vmem, vmem),
        scratch_shapes=[pltpu.VMEM((options, n, n), F32)],
        name="factor",
    )(weights, x, labels)


def split(v):
    high = v.astype(BF16)
    return high, (v - high.astype(F32)).astype(BF16)


def apply_kernel(
    place_ref, weights_ref, xt_ref, xc_ref, label_ref, choice_ref, w_ref, k_ref, *refs
):
    y_refs, (trail_ref, right_ref, khl_ref, y_ref) = refs[:-4], refs[-4:]
    options, groups = weights_ref.shape
    rows, time = xt_ref.shape
    width = xc_ref.shape[1]
    part = time // len(y_refs)
    step = pl.program_id(0)
    row_start, column_start, tm = place_ref[0], place_ref[1], place_ref[2]

    @pl.when(step == 0)
    def _():
        for r in range(options):
            khl_ref[r, 0], khl_ref[r, 1] = split(k_ref[r])

    def product(a_ref, b):
        return jnp.dot(a_ref[0], b, preferred_element_type=F32) + jnp.dot(
            a_ref[1], b, preferred_element_type=F32
        )

    def write(out_ref, z, scale):
        high, low = split(z * scale)
        xt = xt_ref[...]
        out_ref[...] = jnp.dot(xt, high, preferred_element_type=F32) + jnp.dot(
            xt, low, preferred_element_type=F32
        )

    @pl.when(step < options)
    def _():
        out_ref = trail_ref.at[0]

        @pl.when(column_start == 0)
        def _():
            out_ref[...] = jnp.zeros_like(out_ref)

        @pl.when(column_start > 0)
        def _():
            write(out_ref, product(khl_ref.at[step], xc_ref[...]), 1.0 / time)

            @pl.when((column_start >= row_start) & (column_start < row_start + rows))
            def _():
                at = pl.ds(pl.multiple_of(column_start - row_start, B), width)
                ridge = jnp.zeros((1, width), F32)
                for g in range(groups):
                    ridge = jnp.where(label_ref[...] == g, weights_ref[step, g], ridge)
                row = lax.broadcasted_iota(jnp.int32, (width, width), 0)
                col = lax.broadcasted_iota(jnp.int32, (width, width), 1)
                out_ref[at, :] += jnp.where(row == col, ridge, 0.0)

            @pl.when(row_start == 0)
            def _():
                out_ref[:width, :] = jnp.zeros((width, width), F32)

    @pl.when(step >= options)
    def _():
        n = len(y_refs)
        for s in range(n):
            at = pl.ds(pl.multiple_of(lax.rem(tm - s + n, n) * part, part), part)
            y_ref[at, :] = y_refs[s][...]
        y = y_ref[...]
        choice = choice_ref[...]
        z = product(khl_ref.at[0], y)
        for r in range(1, options):
            z = jnp.where(choice == r, product(khl_ref.at[r], y), z)
        write(right_ref, z, time**-0.5)

        @pl.when(row_start == 0)
        def _():
            for r in range(options):
                high, low = split(w_ref[r])
                v = jnp.dot(high, y, preferred_element_type=F32) + jnp.dot(
                    low, y, preferred_element_type=F32
                )
                solved = v if r == 0 else jnp.where(choice == r, v, solved)
            right_ref[:width, :] = solved


def apply(place, weights, xt, xc, labels, choice, w, k, ys):
    rows, time = xt.shape
    width = xc.shape[1]
    voxels = ys[0].shape[1]
    options = weights.shape[0]
    tile = min(512, voxels)
    smem = pl.BlockSpec(memory_space=pltpu.SMEM)
    vmem = pl.BlockSpec(memory_space=pltpu.VMEM)

    def along(s):
        return (0, jnp.maximum(s - options, 0))

    return pl.pallas_call(
        apply_kernel,
        grid=(options + voxels // tile,),
        out_shape=(
            jax.ShapeDtypeStruct((options, rows, width), F32),
            jax.ShapeDtypeStruct((rows, voxels), F32),
        ),
        in_specs=[smem, smem, vmem, vmem, vmem, pl.BlockSpec((1, tile), along), vmem, vmem]
        + [pl.BlockSpec((y.shape[0], tile), along) for y in ys],
        out_specs=(
            pl.BlockSpec((1, rows, width), lambda s: (jnp.minimum(s, options - 1), 0, 0)),
            pl.BlockSpec((rows, tile), along),
        ),
        scratch_shapes=[
            pltpu.VMEM((options, 2, time, time), BF16),
            pltpu.VMEM((time, tile), BF16),
        ],
        name="apply",
    )(place, weights, xt, xc, labels, choice, w, k, *ys)


def local(
    design_matrix, measured_signals, predictor_group_label, shrinkage_weights, target_shrink_choice
):
    nt, nv, nf = (lax.axis_size(a) for a in AXES)
    members = nt * nf
    tm, vox = lax.axis_index("tm"), lax.axis_index("vox")
    member = lax.axis_index(("tm", "feat"))
    rows = design_matrix.shape[1]
    width = predictor_group_label.shape[0]

    def device(g, v):
        return (g // nf * nv + v) * nf + g % nf

    def share(block, owner, mine):
        out = block
        for s in range(1, members):
            pairs = [(device(owner(v), v), device((owner(v) + s) % members, v)) for v in range(nv)]
            got = lax.ppermute(block, AXES, pairs)
            out = jnp.where((member - mine + members) % members == s, got, out)
        return out

    labels = predictor_group_label
    stride = nv
    while stride > 1:
        half = stride // 2
        got = lax.ppermute(labels, "vox", [(a, a + half) for a in range(0, nv, stride)])
        labels = jnp.where(vox % stride == half, got, labels)
        stride = half

    first = share(design_matrix[:, :width], lambda v: 0, 0)
    source = vox * width // rows
    own = lax.dynamic_slice_in_dim(design_matrix, vox * width - source * rows, width, 1)
    columns = share(own, lambda v: v * width // rows, source)
    ys = [measured_signals]
    for s in range(1, nt):
        ys.append(lax.ppermute(measured_signals, "tm", [(a, (a + s) % nt) for a in range(nt)]))

    w, k = factor(shrinkage_weights, first, labels[None, :])
    place = jnp.stack([member * rows, vox * width, tm]).astype(jnp.int32)
    choice = jnp.repeat(target_shrink_choice, GROUP)[None, :]
    return apply(
        place,
        shrinkage_weights,
        design_matrix.T,
        columns,
        predictor_group_label[None, :],
        choice,
        w,
        k,
        ys,
    )


def solution(mesh):
    return jax.shard_map(
        local,
        mesh=mesh,
        in_specs=(P(None, ("tm", "feat")), P("tm", "vox"), P("vox"), P(), P("vox")),
        out_specs=(P(None, ("tm", "feat"), "vox"), P(("tm", "feat"), "vox")),
        check_vma=False,
    )
```

```python
import jax
import jax.numpy as jnp
from jax import lax
from jax.experimental import pallas as pl
from jax.experimental.pallas import tpu as pltpu
from jax.sharding import PartitionSpec as P

GROUP = 64
F32 = jnp.float32
BF16 = jnp.bfloat16
HI = lax.Precision.HIGHEST
FIRST = (((0,), (0,)), ((), ()))
LANES = 128
B = 64
AXES = ("tm", "vox", "feat")


def lane_b(v, index):
    return jnp.take_along_axis(v, index, axis=1, mode="promise_in_bounds")


def sub_b(v, row):
    return jnp.broadcast_to(v[row : row + 1, :], v.shape)


def inverse_factors(tile):
    n = B // 8
    lanes = lax.broadcasted_iota(jnp.int32, (8, LANES), 1)
    subs = lax.broadcasted_iota(jnp.int32, (8, LANES), 0)
    base = jnp.where(lanes < B, 0, B)
    lane = lanes - base
    st = [tile[8 * i : 8 * i + 8, :] for i in range(n)]
    done = []
    for s in range(n):
        index = [base + (8 * s + j) for j in range(8)]
        pivot = (lane >= 8 * s) & (lane < 8 * s + 8)
        c = [lane_b(st[s], index[j]) for j in range(8)]
        row = jnp.where(pivot, jnp.where(lane - 8 * s == subs, 1.0, 0.0), st[s])
        out = row
        for j in range(8):
            d = sub_b(c[j], j)
            recip = 1.0 / d
            here = subs == j
            rb = sub_b(row, j)
            out = jnp.where(here, rb * lax.rsqrt(d), out)
            scaled = rb * recip
            row = jnp.where(here, scaled, row - c[j] * scaled)
            for l in range(j + 1, 8):
                scaled = sub_b(c[l], j) * recip
                c[l] = jnp.where(here, scaled, c[l] - c[j] * scaled)
        done.append(jnp.where(lane < 8 * s + 8, out, 0.0))
        if s + 1 < n:
            v = [sub_b(row, j) for j in range(8)]
            for t in range(s + 1, n):
                acc = jnp.where(pivot, 0.0, st[t])
                for j in range(8):
                    acc = acc - lane_b(st[t], index[j]) * v[j]
                st[t] = acc
    return jnp.concatenate(done, axis=0)


def split3(v):
    high = v.astype(BF16)
    rest = v - high.astype(F32)
    mid = rest.astype(BF16)
    return high, mid, (rest - mid.astype(F32)).astype(BF16)


def factor_kernel(weights_ref, own_ref, mine_ref, last_ref, *refs):
    firsts, (w_ref, k_ref, xt_ref, x_ref, label_ref) = refs[:-5], refs[-5:]
    member = lax.axis_index(("tm", "feat"))
    vox = lax.axis_index("vox")
    width = mine_ref.shape[1]

    @pl.when(member == 0)
    def _():
        x_ref[...] = own_ref[:, :width]

    for s in range(len(firsts)):

        @pl.when(member == s + 1)
        def _():
            x_ref[...] = firsts[s][...]

    label_ref[...] = jnp.where(lax.rem(vox, 2) == 1, last_ref[...], mine_ref[...])

    groups = weights_ref.shape[1]
    time, width = x_ref.shape
    blocks = width // B
    iota = lambda d, shape: lax.broadcasted_iota(jnp.int32, shape, d)
    eye = jnp.where(iota(0, (time, time)) == iota(1, (time, time)), 1.0, 0.0)
    xt_ref[...] = lax.dot_general(x_ref[...], eye.astype(BF16), FIRST, preferred_element_type=F32).astype(BF16)
    low = iota(1, (B, LANES)) < B
    diagonal = iota(1, (B, LANES)) - jnp.where(low, 0, B) == iota(0, (B, LANES))

    def rows(n):
        return slice(n * B, (n + 1) * B)

    def chunk(n):
        return slice(n // 2 * LANES, (n // 2 + 1) * LANES)

    def pair(first, second, n):
        move = 1 - n % 2
        both = [first, second]
        both[move] = pltpu.roll(both[move], B, 1)
        return both

    def ridge(n):
        label = jnp.broadcast_to(label_ref[:, chunk(n)], (8, LANES))
        both = []
        for r in range(2):
            value = jnp.zeros((8, LANES), F32)
            for g in range(groups):
                value = jnp.where(label == g, weights_ref[r, g], value)
            both.append(value)
        both = pair(*both, n)
        return jnp.where(diagonal, jnp.where(low, both[0][:1], both[1][:1]), 0.0)

    def thrice(left, right):
        parts = [jnp.dot(left, p, preferred_element_type=F32) for p in split3(right)]
        return parts[0] + (parts[1] + parts[2])

    def thrice_left(left, right):
        m = left.shape[0]
        parts = jnp.dot(jnp.concatenate(split3(left), axis=0), right, preferred_element_type=F32)
        return parts[:m] + (parts[m : 2 * m] + parts[2 * m :])

    def schur(n, products):
        both = pair(*products, n)
        return jnp.where(low, both[0], both[1]) * (1.0 / time) + ridge(n)

    def coupling(n, products):
        both = pair(*products, n)
        return jnp.concatenate(
            [jnp.where(low, both[0], 0.0), jnp.where(low, 0.0, both[1])], axis=0
        ) * (1.0 / time)

    zeros = jnp.zeros((B, time), F32)
    gram = jnp.dot(xt_ref[rows(0), :], x_ref[:, chunk(0)], preferred_element_type=F32)
    tile = schur(0, [gram, gram])
    xt = xt_ref[: 2 * B, :]
    both = jnp.dot(xt, x_ref[:, chunk(1)], preferred_element_type=F32)
    q = [xt[:B].astype(F32)] * 2
    across = coupling(1, [both[:B]] * 2)
    ahead = schur(1, [both[B:]] * 2)
    for n in range(blocks):
        inverse = inverse_factors(tile)
        if n + 1 < blocks:
            p = jnp.dot(inverse, across, precision=HI, preferred_element_type=F32)
            pp = lax.dot_general(p, p, FIRST, precision=HI, preferred_element_type=F32)
            tile = ahead - jnp.where(low, pp[:B], pp[B:])
        for r in range(2):
            rhs = jnp.concatenate([q[0], zeros] if r == 0 else [zeros, q[1]], axis=0)
            w = jnp.dot(inverse, rhs, precision=HI, preferred_element_type=F32) * time**-0.5
            w_ref[r, rows(n), :] = w
            ww = lax.dot_general(w, w, FIRST, precision=HI, preferred_element_type=F32)
            k_ref[r] = (eye if n == 0 else k_ref[r]) - ww
        if n + 1 < blocks:
            last = n + 2 >= blocks
            xt = xt_ref[(n + 1) * B : (n + (2 if last else 3)) * B, :]
            qq = [thrice(xt, k_ref[r]) for r in range(2)]
            q = [v[:B] for v in qq]
            if not last:
                both = [thrice_left(v, x_ref[:, chunk(n + 2)]) for v in qq]
                across = coupling(n + 2, [v[:B] for v in both])
                ahead = schur(n + 2, [v[B:] for v in both])


def factor(weights, x, labels, last, firsts):
    time = x.shape[0]
    width = labels.shape[1]
    options = weights.shape[0]
    vmem = pl.BlockSpec(memory_space=pltpu.VMEM)
    return pl.pallas_call(
        factor_kernel,
        out_shape=(
            jax.ShapeDtypeStruct((options, width, time), F32),
            jax.ShapeDtypeStruct((options, time, time), F32),
        ),
        in_specs=[pl.BlockSpec(memory_space=pltpu.SMEM)] + [vmem] * (3 + len(firsts)),
        out_specs=(vmem, vmem),
        scratch_shapes=[
            pltpu.VMEM((width, time), BF16),
            pltpu.VMEM((time, width), BF16),
            pltpu.VMEM((1, width), jnp.int32),
        ],
        name="factor",
    )(weights, x, labels, last, *firsts)


def split(v):
    high = v.astype(BF16)
    return high, (v - high.astype(F32)).astype(BF16)


def apply_kernel(members, weights_ref, choice_ref, x_ref, label_ref, w_ref, k_ref, *refs):
    got_refs, y_refs = refs[: members - 1], refs[members - 1 : -7]
    trail_ref, right_ref, xt_ref, xc_ref, ks_ref, ws_ref, ym_ref = refs[-7:]
    options, groups = weights_ref.shape
    time, rows = x_ref.shape
    width = xc_ref.shape[1]
    tile = right_ref.shape[1]
    part = time // len(y_refs)
    step = pl.program_id(0)
    member = lax.axis_index(("tm", "feat"))
    vox = lax.axis_index("vox")
    tm = lax.axis_index("tm")
    owner = vox * width // rows
    offset = vox * width - owner * rows

    @pl.when(step == 0)
    def _():
        eye = lax.broadcasted_iota(jnp.int32, (time, time), 0) == lax.broadcasted_iota(
            jnp.int32, (time, time), 1
        )
        eye = jnp.where(eye, 1.0, 0.0).astype(BF16)
        xt = lax.dot_general(x_ref[...], eye, FIRST, preferred_element_type=F32).astype(BF16)
        xt_ref[:, :time] = xt
        xt_ref[:, time:] = xt
        for r in range(options):
            at = slice(2 * r * time, (2 * r + 1) * time), slice((2 * r + 1) * time, (2 * r + 2) * time)
            ks_ref[:, at[0]], ks_ref[:, at[1]] = split(k_ref[r])

            @pl.when(member == 0)
            def _():
                ws_ref[:, at[0]], ws_ref[:, at[1]] = split(w_ref[r])

        @pl.when(owner == member)
        def _():
            xc_ref[...] = x_ref[:, pl.ds(pl.multiple_of(offset, LANES), width)]

        for s in range(1, members):

            @pl.when(lax.rem(member - owner + members, members) == s)
            def _():
                xc_ref[...] = got_refs[s - 1][...]

    def write(out_ref, z):
        zs = jnp.concatenate(split(z), axis=0)

        @pl.when(member == 0)
        def _():
            out_ref[width:, :] = jnp.dot(xt_ref[width:, :], zs, preferred_element_type=F32)

        @pl.when(member > 0)
        def _():
            out_ref[...] = jnp.dot(xt_ref[...], zs, preferred_element_type=F32)

    @pl.when(step < options)
    def _():
        out_ref = trail_ref.at[0]

        @pl.when(vox == 0)
        def _():
            out_ref[...] = jnp.zeros_like(out_ref)

        @pl.when(vox > 0)
        def _():
            at = pl.ds(pl.multiple_of(step * 2 * time, LANES), 2 * time)
            xc = xc_ref[...]
            z = jnp.dot(ks_ref[:, at], jnp.concatenate([xc, xc], axis=0), preferred_element_type=F32)
            write(out_ref, z * (1.0 / time))

            @pl.when(member == 0)
            def _():
                out_ref[:width, :] = jnp.zeros((width, width), F32)

            @pl.when(owner == member)
            def _():
                to = pl.ds(pl.multiple_of(offset, LANES), width)
                ridge = jnp.zeros((1, width), F32)
                for g in range(groups):
                    ridge = jnp.where(label_ref[...] == g, weights_ref[step, g], ridge)
                row = lax.broadcasted_iota(jnp.int32, (width, width), 0)
                col = lax.broadcasted_iota(jnp.int32, (width, width), 1)
                out_ref[to, :] += jnp.where(row == col, ridge, 0.0)

    @pl.when(step >= options)
    def _():
        n = len(y_refs)
        start = (step - options) * tile
        lane = lax.broadcasted_iota(jnp.int32, (1, LANES), 1)
        chosen = []
        for c in range(tile // LANES):
            value = jnp.zeros((1, LANES), F32)
            for i in range(LANES // GROUP):
                choice = choice_ref[start // GROUP + c * (LANES // GROUP) + i].astype(F32)
                value = jnp.where(lane >= i * GROUP, choice, value)
            chosen.append(value)
        chosen = jnp.concatenate(chosen, axis=1)
        for s in range(n):
            y = y_refs[s][:, pl.ds(pl.multiple_of(start, LANES), tile)].astype(F32)
            for r in range(options):
                masked = jnp.where(chosen == float(r), y, 0.0).astype(BF16)
                for h in range(2):
                    to = (2 * r + h) * time + lax.rem(tm - s + n, n) * part
                    ym_ref[pl.ds(pl.multiple_of(to, part), part), :] = masked
        ym = ym_ref[...]
        write(right_ref, jnp.dot(ks_ref[...], ym, preferred_element_type=F32) * time**-0.5)

        @pl.when(member == 0)
        def _():
            right_ref[:width, :] = jnp.dot(ws_ref[...], ym, preferred_element_type=F32)


def apply(weights, choice, x, labels, w, k, gots, ys):
    time, rows = x.shape
    width = labels.shape[1]
    voxels = ys[0].shape[1]
    options = weights.shape[0]
    tile = min(512, voxels)
    smem = pl.BlockSpec(memory_space=pltpu.SMEM)
    vmem = pl.BlockSpec(memory_space=pltpu.VMEM)
    return pl.pallas_call(
        lambda *refs: apply_kernel(len(gots) + 1, *refs),
        grid=(options + voxels // tile,),
        out_shape=(
            jax.ShapeDtypeStruct((options, rows, width), F32),
            jax.ShapeDtypeStruct((rows, voxels), F32),
        ),
        in_specs=[smem, smem] + [vmem] * (4 + len(gots) + len(ys)),
        out_specs=(
            pl.BlockSpec((1, rows, width), lambda s: (jnp.minimum(s, options - 1), 0, 0)),
            pl.BlockSpec((rows, tile), lambda s: (0, jnp.maximum(s - options, 0))),
        ),
        scratch_shapes=[
            pltpu.VMEM((rows, 2 * time), BF16),
            pltpu.VMEM((time, width), BF16),
            pltpu.VMEM((time, 2 * options * time), BF16),
            pltpu.VMEM((width, 2 * options * time), BF16),
            pltpu.VMEM((2 * options * time, tile), BF16),
        ],
        name="apply",
    )(weights, choice, x, labels, w, k, *gots, *ys)


def local(
    design_matrix, measured_signals, predictor_group_label, shrinkage_weights, target_shrink_choice
):
    nt, nv, nf = (lax.axis_size(a) for a in AXES)
    members = nt * nf
    vox = lax.axis_index("vox")
    rows = design_matrix.shape[1]
    width = predictor_group_label.shape[0]

    def device(g, v):
        return (g // nf * nv + v) * nf + g % nf

    def share(block, owner):
        gots = []
        for s in range(1, members):
            pairs = [(device(owner(v), v), device((owner(v) + s) % members, v)) for v in range(nv)]
            gots.append(lax.ppermute(block, AXES, pairs))
        return gots

    firsts = share(design_matrix[:, :width], lambda v: 0)
    labels = predictor_group_label[None, :]
    stride = nv
    while stride > 1:
        half = stride // 2
        got = lax.ppermute(labels, "vox", [(a, a + half) for a in range(0, nv, stride)])
        if half > 1:
            labels = jnp.where(vox % stride == half, got, labels)
        stride = half

    source = vox * width // rows
    own = lax.dynamic_slice_in_dim(design_matrix, vox * width - source * rows, width, 1)
    columns = share(own, lambda v: v * width // rows)
    ys = [measured_signals]
    for s in range(1, nt):
        ys.append(lax.ppermute(measured_signals, "tm", [(a, (a + s) % nt) for a in range(nt)]))

    w, k = factor(shrinkage_weights, design_matrix, labels, got, firsts)
    return apply(
        shrinkage_weights,
        target_shrink_choice,
        design_matrix,
        predictor_group_label[None, :],
        w,
        k,
        columns,
        ys,
    )


def solution(mesh):
    return jax.shard_map(
        local,
        mesh=mesh,
        in_specs=(P(None, ("tm", "feat")), P("tm", "vox"), P("vox"), P(), P("vox")),
        out_specs=(P(None, ("tm", "feat"), "vox"), P(("tm", "feat"), "vox")),
        check_vma=False,
    )
```

```python
import jax
import jax.numpy as jnp
from jax import lax
from jax.experimental import pallas as pl
from jax.experimental.pallas import tpu as pltpu
from jax.sharding import PartitionSpec as P

GROUP = 64
F32 = jnp.float32
BF16 = jnp.bfloat16
HI = lax.Precision.HIGHEST
FIRST = (((0,), (0,)), ((), ()))
LANES = 128
B = 64
AXES = ("tm", "vox", "feat")


def lane_b(v, index):
    return jnp.take_along_axis(v, index, axis=1, mode="promise_in_bounds")


def sub_b(v, row):
    return jnp.broadcast_to(v[row : row + 1, :], v.shape)


def inverse_factors(tile):
    n = B // 8
    lanes = lax.broadcasted_iota(jnp.int32, (8, LANES), 1)
    subs = lax.broadcasted_iota(jnp.int32, (8, LANES), 0)
    base = jnp.where(lanes < B, 0, B)
    lane = lanes - base
    st = [tile[8 * i : 8 * i + 8, :] for i in range(n)]
    done = []
    for s in range(n):
        index = [base + (8 * s + j) for j in range(8)]
        pivot = (lane >= 8 * s) & (lane < 8 * s + 8)
        c = [lane_b(st[s], index[j]) for j in range(8)]
        row = jnp.where(pivot, jnp.where(lane - 8 * s == subs, 1.0, 0.0), st[s])
        out = row
        for j in range(8):
            d = sub_b(c[j], j)
            recip = 1.0 / d
            here = subs == j
            rb = sub_b(row, j)
            out = jnp.where(here, rb * lax.rsqrt(d), out)
            scaled = rb * recip
            row = jnp.where(here, scaled, row - c[j] * scaled)
            for l in range(j + 1, 8):
                scaled = sub_b(c[l], j) * recip
                c[l] = jnp.where(here, scaled, c[l] - c[j] * scaled)
        done.append(jnp.where(lane < 8 * s + 8, out, 0.0))
        if s + 1 < n:
            v = [sub_b(row, j) for j in range(8)]
            for t in range(s + 1, n):
                acc = jnp.where(pivot, 0.0, st[t])
                for j in range(8):
                    acc = acc - lane_b(st[t], index[j]) * v[j]
                st[t] = acc
    return jnp.concatenate(done, axis=0)


def split3(v):
    high = v.astype(BF16)
    rest = v - high.astype(F32)
    mid = rest.astype(BF16)
    return high, mid, (rest - mid.astype(F32)).astype(BF16)


def resident(v):
    return pltpu.with_memory_space_constraint(v, pltpu.VMEM)


def split(v):
    high = v.astype(BF16)
    return high, (v - high.astype(F32)).astype(BF16)


def factor_kernel(weights_ref, own_ref, mine_ref, last_ref, *refs):
    firsts, refs = refs[:-11], refs[-11:]
    w_out, k_out, xt_out = refs[:3]
    ws_ref, ks_ref, k_ref, xt_ref, x_ref, label_ref, xo_ref, sems = refs[3:]
    member = lax.axis_index(("tm", "feat"))
    vox = lax.axis_index("vox")
    width = mine_ref.shape[1]

    @pl.when(member == 0)
    def _():
        x_ref[...] = own_ref[:, :width]

    for s in range(len(firsts)):

        @pl.when(member == s + 1)
        def _():
            pltpu.sync_copy(firsts[s], x_ref)

    @pl.when(lax.rem(vox, 2) == 1)
    def _():
        pltpu.sync_copy(last_ref, label_ref)

    @pl.when(lax.rem(vox, 2) == 0)
    def _():
        pltpu.sync_copy(mine_ref, label_ref)

    groups = weights_ref.shape[1]
    time = x_ref.shape[0]
    blocks = width // B
    copies = []

    def send(source, target):
        copies.append(pltpu.make_async_copy(source, target, sems.at[len(copies)]))
        copies[-1].start()

    iota = lambda d, shape: lax.broadcasted_iota(jnp.int32, shape, d)
    eye = jnp.where(iota(0, (time, time)) == iota(1, (time, time)), 1.0, 0.0)
    xt_ref[...] = lax.dot_general(
        x_ref[...], eye.astype(BF16), FIRST, preferred_element_type=F32
    ).astype(BF16)
    low = iota(1, (B, LANES)) < B
    diagonal = iota(1, (B, LANES)) - jnp.where(low, 0, B) == iota(0, (B, LANES))

    def rows(n):
        return slice(n * B, (n + 1) * B)

    def chunk(n):
        return slice(n // 2 * LANES, (n // 2 + 1) * LANES)

    def pair(first, second, n):
        move = 1 - n % 2
        both = [first, second]
        both[move] = pltpu.roll(both[move], B, 1)
        return both

    def ridge(n):
        label = jnp.broadcast_to(label_ref[:, chunk(n)], (8, LANES))
        both = []
        for r in range(2):
            value = jnp.zeros((8, LANES), F32)
            for g in range(groups):
                value = jnp.where(label == g, weights_ref[r, g], value)
            both.append(value)
        both = pair(*both, n)
        return jnp.where(diagonal, jnp.where(low, both[0][:1], both[1][:1]), 0.0)

    def thrice(left, right):
        parts = [jnp.dot(left, p, preferred_element_type=F32) for p in split3(right)]
        return parts[0] + (parts[1] + parts[2])

    def thrice_left(left, right):
        m = left.shape[0]
        parts = jnp.dot(jnp.concatenate(split3(left), axis=0), right, preferred_element_type=F32)
        return parts[:m] + (parts[m : 2 * m] + parts[2 * m :])

    def schur(n, products):
        both = pair(*products, n)
        return jnp.where(low, both[0], both[1]) * (1.0 / time) + ridge(n)

    def coupling(n, products):
        both = pair(*products, n)
        return jnp.concatenate(
            [jnp.where(low, both[0], 0.0), jnp.where(low, 0.0, both[1])], axis=0
        ) * (1.0 / time)

    zeros = jnp.zeros((B, time), F32)
    gram = jnp.dot(xt_ref[rows(0), :], x_ref[:, chunk(0)], preferred_element_type=F32)
    tile = schur(0, [gram, gram])
    xt = xt_ref[: 2 * B, :]
    both = jnp.dot(xt, x_ref[:, chunk(1)], preferred_element_type=F32)
    q = [xt[:B].astype(F32)] * 2
    across = coupling(1, [both[:B]] * 2)
    ahead = schur(1, [both[B:]] * 2)
    for n in range(blocks):
        inverse = inverse_factors(tile)
        if n + 1 < blocks:
            p = jnp.dot(inverse, across, precision=HI, preferred_element_type=F32)
            pp = lax.dot_general(p, p, FIRST, precision=HI, preferred_element_type=F32)
            tile = ahead - jnp.where(low, pp[:B], pp[B:])
        for r in range(2):
            rhs = jnp.concatenate([q[0], zeros] if r == 0 else [zeros, q[1]], axis=0)
            w = jnp.dot(inverse, rhs, precision=HI, preferred_element_type=F32) * time**-0.5
            at = 2 * r * time
            ws_ref[rows(n), at : at + time], ws_ref[rows(n), at + time : at + 2 * time] = split(w)
            ww = lax.dot_general(w, w, FIRST, precision=HI, preferred_element_type=F32)
            k_ref[r] = (eye if n == 0 else k_ref[r]) - ww
        if n == 0:
            xo_ref[...] = lax.dot_general(
                own_ref[...], eye.astype(BF16), FIRST, preferred_element_type=F32
            ).astype(BF16)
        if n + 1 < blocks:
            last = n + 2 >= blocks
            xt = xt_ref[(n + 1) * B : (n + (2 if last else 3)) * B, :]
            qq = [thrice(xt, k_ref[r]) for r in range(2)]
            q = [v[:B] for v in qq]
            if not last:
                both = [thrice_left(v, x_ref[:, chunk(n + 2)]) for v in qq]
                across = coupling(n + 2, [v[:B] for v in both])
                ahead = schur(n + 2, [v[B:] for v in both])
    for r in range(2):
        at = 2 * r * time
        ks_ref[:, at : at + time], ks_ref[:, at + time : at + 2 * time] = split(k_ref[r])
    send(ks_ref, k_out)
    send(xo_ref, xt_out)

    @pl.when(member == 0)
    def _():
        pltpu.sync_copy(ws_ref, w_out)

    for c in copies:
        c.wait()


def factor(weights, x, labels, last, firsts):
    time, rows = x.shape
    width = labels.shape[1]
    stack = 2 * weights.shape[0] * time
    vmem = pl.BlockSpec(memory_space=pltpu.VMEM)
    hbm = pl.BlockSpec(memory_space=pl.ANY)
    return pl.pallas_call(
        factor_kernel,
        out_shape=(
            jax.ShapeDtypeStruct((width, stack), BF16),
            jax.ShapeDtypeStruct((time, stack), BF16),
            jax.ShapeDtypeStruct((rows, time), BF16),
        ),
        in_specs=[pl.BlockSpec(memory_space=pltpu.SMEM), vmem, hbm, hbm] + [hbm] * len(firsts),
        out_specs=(hbm, hbm, hbm),
        scratch_shapes=[
            pltpu.VMEM((width, stack), BF16),
            pltpu.VMEM((time, stack), BF16),
            pltpu.VMEM((2, time, time), F32),
            pltpu.VMEM((width, time), BF16),
            pltpu.VMEM((time, width), BF16),
            pltpu.VMEM((1, width), jnp.int32),
            pltpu.VMEM((rows, time), BF16),
            pltpu.SemaphoreType.DMA((2,)),
        ],
        name="factor",
    )(weights, x, labels, last, *firsts)


def apply_kernel(members, weights_ref, choice_ref, label_ref, x_hbm, xt_hbm, w_hbm, k_hbm, *refs):
    got_refs, y_hbms = refs[: members - 1], refs[members - 1 : -9]
    trail_ref, right_ref, xt_ref, xc_ref, ks_ref, ws_ref, y_ref, ym_ref, sems = refs[-9:]
    options, groups = weights_ref.shape
    rows = xt_hbm.shape[0]
    time, width = xc_ref.shape
    tile = right_ref.shape[1]
    n = len(y_hbms)
    part = time // n
    step = pl.program_id(0)
    member = lax.axis_index(("tm", "feat"))
    vox = lax.axis_index("vox")
    tm = lax.axis_index("tm")
    owner = vox * width // rows
    offset = vox * width - owner * rows

    early = [
        pltpu.make_async_copy(k_hbm, ks_ref, sems.at[0]),
        pltpu.make_async_copy(xt_hbm, xt_ref, sems.at[1]),
    ]
    late = [
        pltpu.make_async_copy(
            y_hbms[s],
            y_ref.at[pl.ds(pl.multiple_of(lax.rem(tm - s + n, n) * part, part), part), :],
            sems.at[2 + s],
        )
        for s in range(n)
    ]
    rest = pltpu.make_async_copy(w_hbm, ws_ref, sems.at[2 + n])

    @pl.when(step == 0)
    def _():
        for c in early + late:
            c.start()

        @pl.when(member == 0)
        def _():
            rest.start()

        @pl.when(owner == member)
        def _():
            pltpu.sync_copy(x_hbm.at[:, pl.ds(pl.multiple_of(offset, LANES), width)], xc_ref)

        for s in range(1, members):

            @pl.when(lax.rem(member - owner + members, members) == s)
            def _():
                pltpu.sync_copy(got_refs[s - 1], xc_ref)

        for c in early:
            c.wait()

    @pl.when(step == options)
    def _():
        for c in late:
            c.wait()

        @pl.when(member == 0)
        def _():
            rest.wait()

    def write(out_ref, z):
        high, low = split(z)

        def product(xt):
            return jnp.dot(xt, high, preferred_element_type=F32) + jnp.dot(
                xt, low, preferred_element_type=F32
            )

        @pl.when(member == 0)
        def _():
            out_ref[width:, :] = product(xt_ref[width:, :])

        @pl.when(member > 0)
        def _():
            out_ref[...] = product(xt_ref[...])

    @pl.when(step < options)
    def _():
        out_ref = trail_ref.at[0]

        @pl.when(vox == 0)
        def _():
            out_ref[...] = jnp.zeros_like(out_ref)

        @pl.when(vox > 0)
        def _():
            at = pl.ds(pl.multiple_of(step * 2 * time, LANES), 2 * time)
            xc = xc_ref[...]
            z = jnp.dot(ks_ref[:, at], jnp.concatenate([xc, xc], axis=0), preferred_element_type=F32)
            write(out_ref, z * (1.0 / time))

            @pl.when(member == 0)
            def _():
                out_ref[:width, :] = jnp.zeros((width, width), F32)

            @pl.when(owner == member)
            def _():
                to = pl.ds(pl.multiple_of(offset, LANES), width)
                ridge = jnp.zeros((1, width), F32)
                for g in range(groups):
                    ridge = jnp.where(label_ref[...] == g, weights_ref[step, g], ridge)
                row = lax.broadcasted_iota(jnp.int32, (width, width), 0)
                col = lax.broadcasted_iota(jnp.int32, (width, width), 1)
                out_ref[to, :] += jnp.where(row == col, ridge, 0.0)

    @pl.when(step >= options)
    def _():
        start = (step - options) * tile
        lane = lax.broadcasted_iota(jnp.int32, (1, LANES), 1)
        chosen = []
        for c in range(tile // LANES):
            value = jnp.zeros((1, LANES), F32)
            for i in range(LANES // GROUP):
                choice = choice_ref[start // GROUP + c * (LANES // GROUP) + i].astype(F32)
                value = jnp.where(lane >= i * GROUP, choice, value)
            chosen.append(value)
        chosen = jnp.concatenate(chosen, axis=1)
        y = y_ref[:, pl.ds(pl.multiple_of(start, LANES), tile)].astype(F32)
        for r in range(options):
            masked = jnp.where(chosen == float(r), y, 0.0).astype(BF16)
            for h in range(2):
                to = (2 * r + h) * time
                ym_ref[to : to + time, :] = masked
        ym = ym_ref[...]
        write(right_ref, jnp.dot(ks_ref[...], ym, preferred_element_type=F32) * time**-0.5)

        @pl.when(member == 0)
        def _():
            right_ref[:width, :] = jnp.dot(ws_ref[...], ym, preferred_element_type=F32)


def apply(weights, choice, labels, x, xt, w, k, gots, ys):
    rows, time = xt.shape
    width = labels.shape[1]
    voxels = ys[0].shape[1]
    options = weights.shape[0]
    tile = min(512, voxels)
    stack = 2 * options * time
    smem = pl.BlockSpec(memory_space=pltpu.SMEM)
    vmem = pl.BlockSpec(memory_space=pltpu.VMEM)
    hbm = pl.BlockSpec(memory_space=pl.ANY)
    return pl.pallas_call(
        lambda *refs: apply_kernel(len(gots) + 1, *refs),
        grid=(options + voxels // tile,),
        out_shape=(
            jax.ShapeDtypeStruct((options, rows, width), F32),
            jax.ShapeDtypeStruct((rows, voxels), F32),
        ),
        in_specs=[smem, smem, vmem] + [hbm] * (4 + len(gots) + len(ys)),
        out_specs=(
            pl.BlockSpec((1, rows, width), lambda s: (jnp.minimum(s, options - 1), 0, 0)),
            pl.BlockSpec((rows, tile), lambda s: (0, jnp.maximum(s - options, 0))),
        ),
        scratch_shapes=[
            pltpu.VMEM((rows, time), BF16),
            pltpu.VMEM((time, width), BF16),
            pltpu.VMEM((time, stack), BF16),
            pltpu.VMEM((width, stack), BF16),
            pltpu.VMEM((time, voxels), BF16),
            pltpu.VMEM((stack, tile), BF16),
            pltpu.SemaphoreType.DMA((3 + len(ys),)),
        ],
        name="apply",
    )(weights, choice, labels, x, xt, w, k, *gots, *ys)


def local(
    design_matrix, measured_signals, predictor_group_label, shrinkage_weights, target_shrink_choice
):
    nt, nv, nf = (lax.axis_size(a) for a in AXES)
    members = nt * nf
    vox = lax.axis_index("vox")
    rows = design_matrix.shape[1]
    width = predictor_group_label.shape[0]

    def device(g, v):
        return (g // nf * nv + v) * nf + g % nf

    def share(block, owner):
        gots = []
        for s in range(1, members):
            pairs = [(device(owner(v), v), device((owner(v) + s) % members, v)) for v in range(nv)]
            gots.append(lax.ppermute(block, AXES, pairs))
        small = len(gots) * block.size * block.dtype.itemsize <= 2**20
        return [resident(got) for got in gots] if small else gots

    firsts = share(design_matrix[:, :width], lambda v: 0)
    labels = predictor_group_label[None, :]
    stride = nv
    while stride > 1:
        half = stride // 2
        got = lax.ppermute(labels, "vox", [(a, a + half) for a in range(0, nv, stride)])
        if half > 1:
            labels = jnp.where(vox % stride == half, got, labels)
        stride = half
    ys = [measured_signals]
    for s in range(1, nt):
        pairs = [(a, (a + s) % nt) for a in range(nt)]
        ys.append(resident(lax.ppermute(measured_signals, "tm", pairs)))
    source = vox * width // rows
    own = lax.dynamic_slice_in_dim(design_matrix, vox * width - source * rows, width, 1)
    columns = share(own, lambda v: v * width // rows)

    w, k, xt = factor(
        shrinkage_weights, design_matrix, resident(labels), resident(got), firsts
    )
    return apply(
        shrinkage_weights,
        target_shrink_choice,
        predictor_group_label[None, :],
        design_matrix,
        xt,
        w,
        k,
        columns,
        ys,
    )


def solution(mesh):
    return jax.shard_map(
        local,
        mesh=mesh,
        in_specs=(P(None, ("tm", "feat")), P("tm", "vox"), P("vox"), P(), P("vox")),
        out_specs=(P(None, ("tm", "feat"), "vox"), P(("tm", "feat"), "vox")),
        check_vma=False,
    )
```

```python
import jax
import jax.numpy as jnp
from jax import lax
from jax.experimental import pallas as pl
from jax.experimental.pallas import tpu as pltpu
from jax.sharding import PartitionSpec as P

GROUP = 64
F32 = jnp.float32
BF16 = jnp.bfloat16
FIRST = (((0,), (0,)), ((), ()))
LANES = 128
B = 64
AXES = ("tm", "vox", "feat")


def lane_b(v, index):
    return jnp.take_along_axis(v, index, axis=1, mode="promise_in_bounds")


def sub_b(v, row):
    return jnp.broadcast_to(v[row : row + 1, :], v.shape)


def inverse_factors(tile):
    n = B // 8
    lanes = lax.broadcasted_iota(jnp.int32, (8, LANES), 1)
    subs = lax.broadcasted_iota(jnp.int32, (8, LANES), 0)
    base = jnp.where(lanes < B, 0, B)
    lane = lanes - base
    st = [tile[8 * i : 8 * i + 8, :] for i in range(n)]
    done = []
    for s in range(n):
        index = [base + (8 * s + j) for j in range(8)]
        pivot = (lane >= 8 * s) & (lane < 8 * s + 8)
        c = [lane_b(st[s], index[j]) for j in range(8)]
        row = jnp.where(pivot, jnp.where(lane - 8 * s == subs, 1.0, 0.0), st[s])
        out = row
        for j in range(8):
            d = sub_b(c[j], j)
            recip = 1.0 / d
            here = subs == j
            rb = sub_b(row, j)
            out = jnp.where(here, rb * lax.rsqrt(d), out)
            scaled = rb * recip
            row = jnp.where(here, scaled, row - c[j] * scaled)
            for l in range(j + 1, 8):
                scaled = sub_b(c[l], j) * recip
                c[l] = jnp.where(here, scaled, c[l] - c[j] * scaled)
        done.append(jnp.where(lane < 8 * s + 8, out, 0.0))
        if s + 1 < n:
            v = [sub_b(row, j) for j in range(8)]
            for t in range(s + 1, n):
                acc = jnp.where(pivot, 0.0, st[t])
                for j in range(8):
                    acc = acc - lane_b(st[t], index[j]) * v[j]
                st[t] = acc
    return jnp.concatenate(done, axis=0)


def split3(v):
    high = v.astype(BF16)
    rest = v - high.astype(F32)
    mid = rest.astype(BF16)
    return high, mid, (rest - mid.astype(F32)).astype(BF16)


def resident(v):
    return pltpu.with_memory_space_constraint(v, pltpu.VMEM)


def split(v):
    high = v.astype(BF16)
    return high, (v - high.astype(F32)).astype(BF16)


PRODUCTS = ((0, 0), (0, 1), (1, 0), (0, 2), (2, 0), (1, 1))


def stack(v, side, axis):
    parts = split3(v)
    return jnp.concatenate([parts[p[side]] for p in PRODUCTS], axis=axis)


def factor_kernel(weights_ref, own_ref, mine_ref, last_ref, *refs):
    firsts, refs = refs[:-11], refs[-11:]
    w_out, k_out, xt_out = refs[:3]
    ws_ref, ks_ref, k_ref, xt_ref, x_ref, label_ref, xo_ref, sems = refs[3:]
    member = lax.axis_index(("tm", "feat"))
    vox = lax.axis_index("vox")
    width = mine_ref.shape[1]

    @pl.when(member == 0)
    def _():
        x_ref[...] = own_ref[:, :width]

    for s in range(len(firsts)):

        @pl.when(member == s + 1)
        def _():
            pltpu.sync_copy(firsts[s], x_ref)

    received = 2 * vox >= lax.axis_size("vox")

    @pl.when(received)
    def _():
        pltpu.sync_copy(last_ref, label_ref)

    @pl.when(jnp.logical_not(received))
    def _():
        pltpu.sync_copy(mine_ref, label_ref)

    groups = weights_ref.shape[1]
    time = x_ref.shape[0]
    blocks = width // B
    copies = []

    def send(source, target):
        copies.append(pltpu.make_async_copy(source, target, sems.at[len(copies)]))
        copies[-1].start()

    iota = lambda d, shape: lax.broadcasted_iota(jnp.int32, shape, d)
    eye = jnp.where(iota(0, (time, time)) == iota(1, (time, time)), 1.0, 0.0)
    xt_ref[...] = lax.dot_general(
        x_ref[...], eye.astype(BF16), FIRST, preferred_element_type=F32
    ).astype(BF16)
    low = iota(1, (B, LANES)) < B
    diagonal = iota(1, (B, LANES)) - jnp.where(low, 0, B) == iota(0, (B, LANES))

    def rows(n):
        return slice(n * B, (n + 1) * B)

    def chunk(n):
        return slice(n // 2 * LANES, (n // 2 + 1) * LANES)

    def pair(first, second, n):
        move = 1 - n % 2
        both = [first, second]
        both[move] = pltpu.roll(both[move], B, 1)
        return both

    def ridge(n):
        label = jnp.broadcast_to(label_ref[:, chunk(n)], (8, LANES))
        both = []
        for r in range(2):
            value = jnp.zeros((8, LANES), F32)
            for g in range(groups):
                value = jnp.where(label == g, weights_ref[r, g], value)
            both.append(value)
        both = pair(*both, n)
        return jnp.where(diagonal, jnp.where(low, both[0][:1], both[1][:1]), 0.0)

    def thrice(left, right):
        parts = [jnp.dot(left, p, preferred_element_type=F32) for p in split3(right)]
        return parts[0] + (parts[1] + parts[2])

    def thrice_left(left, right):
        m = left.shape[0]
        parts = jnp.dot(jnp.concatenate(split3(left), axis=0), right, preferred_element_type=F32)
        return parts[:m] + (parts[m : 2 * m] + parts[2 * m :])

    def schur(n, products):
        both = pair(*products, n)
        return jnp.where(low, both[0], both[1]) * (1.0 / time) + ridge(n)

    def coupling(n, products):
        both = pair(*products, n)
        return jnp.concatenate(
            [jnp.where(low, both[0], 0.0), jnp.where(low, 0.0, both[1])], axis=0
        ) * (1.0 / time)

    zeros = jnp.zeros((B, time), F32)
    gram = jnp.dot(xt_ref[rows(0), :], x_ref[:, chunk(0)], preferred_element_type=F32)
    tile = schur(0, [gram, gram])
    xt = xt_ref[: 2 * B, :]
    both = jnp.dot(xt, x_ref[:, chunk(1)], preferred_element_type=F32)
    q = [xt[:B].astype(F32)] * 2
    across = coupling(1, [both[:B]] * 2)
    ahead = schur(1, [both[B:]] * 2)
    for n in range(blocks):
        inverse = stack(inverse_factors(tile), 0, 1)
        if n + 1 < blocks:
            p = jnp.dot(inverse, stack(across, 1, 0), preferred_element_type=F32)
            pp = lax.dot_general(stack(p, 0, 0), stack(p, 1, 0), FIRST, preferred_element_type=F32)
            tile = ahead - jnp.where(low, pp[:B], pp[B:])
        for r in range(2):
            rhs = jnp.concatenate([q[0], zeros] if r == 0 else [zeros, q[1]], axis=0)
            w = jnp.dot(inverse, stack(rhs, 1, 0), preferred_element_type=F32) * time**-0.5
            at = 2 * r * time
            ws_ref[rows(n), at : at + time], ws_ref[rows(n), at + time : at + 2 * time] = split(w)
            ww = lax.dot_general(stack(w, 0, 0), stack(w, 1, 0), FIRST, preferred_element_type=F32)
            k_ref[r] = (eye if n == 0 else k_ref[r]) - ww
        if n == 0:
            xo_ref[...] = lax.dot_general(
                own_ref[...], eye.astype(BF16), FIRST, preferred_element_type=F32
            ).astype(BF16)
        if n + 1 < blocks:
            last = n + 2 >= blocks
            xt = xt_ref[(n + 1) * B : (n + (2 if last else 3)) * B, :]
            qq = [thrice(xt, k_ref[r]) for r in range(2)]
            q = [v[:B] for v in qq]
            if not last:
                both = [thrice_left(v, x_ref[:, chunk(n + 2)]) for v in qq]
                across = coupling(n + 2, [v[:B] for v in both])
                ahead = schur(n + 2, [v[B:] for v in both])
    for r in range(2):
        at = 2 * r * time
        ks_ref[:, at : at + time], ks_ref[:, at + time : at + 2 * time] = split(k_ref[r])
    send(ks_ref, k_out)
    send(xo_ref, xt_out)

    @pl.when(member == 0)
    def _():
        pltpu.sync_copy(ws_ref, w_out)

    for c in copies:
        c.wait()


def factor(weights, x, labels, last, firsts):
    time, rows = x.shape
    width = labels.shape[1]
    stack = 2 * weights.shape[0] * time
    vmem = pl.BlockSpec(memory_space=pltpu.VMEM)
    hbm = pl.BlockSpec(memory_space=pl.ANY)
    return pl.pallas_call(
        factor_kernel,
        out_shape=(
            jax.ShapeDtypeStruct((width, stack), BF16),
            jax.ShapeDtypeStruct((time, stack), BF16),
            jax.ShapeDtypeStruct((rows, time), BF16),
        ),
        in_specs=[pl.BlockSpec(memory_space=pltpu.SMEM), vmem, hbm, hbm] + [hbm] * len(firsts),
        out_specs=(hbm, hbm, hbm),
        scratch_shapes=[
            pltpu.VMEM((width, stack), BF16),
            pltpu.VMEM((time, stack), BF16),
            pltpu.VMEM((2, time, time), F32),
            pltpu.VMEM((width, time), BF16),
            pltpu.VMEM((time, width), BF16),
            pltpu.VMEM((1, width), jnp.int32),
            pltpu.VMEM((rows, time), BF16),
            pltpu.SemaphoreType.DMA((2,)),
        ],
        name="factor",
    )(weights, x, labels, last, *firsts)


def apply_kernel(members, weights_ref, choice_ref, label_ref, x_hbm, xt_hbm, w_hbm, k_hbm, *refs):
    got_refs, y_hbms = refs[: members - 1], refs[members - 1 : -11]
    trail_hbm, right_hbm = refs[-11:-9]
    xt_ref, xc_ref, ks_ref, ws_ref, y_ref, ym_ref, out_ref, sems, sent = refs[-9:]
    options, groups = weights_ref.shape
    tiles, rows, tile = out_ref.shape
    time, width = xc_ref.shape
    n = len(y_hbms)
    part = time // n
    member = lax.axis_index(("tm", "feat"))
    vox = lax.axis_index("vox")
    tm = lax.axis_index("tm")
    owner = vox * width // rows
    offset = vox * width - owner * rows

    early = [
        pltpu.make_async_copy(k_hbm, ks_ref, sems.at[0]),
        pltpu.make_async_copy(xt_hbm, xt_ref, sems.at[1]),
    ]
    late = [
        pltpu.make_async_copy(
            y_hbms[s],
            y_ref.at[pl.ds(pl.multiple_of(lax.rem(tm - s + n, n) * part, part), part), :],
            sems.at[2 + s],
        )
        for s in range(n)
    ]
    rest = pltpu.make_async_copy(w_hbm, ws_ref, sems.at[2 + n])
    for c in early + late:
        c.start()

    @pl.when(member == 0)
    def _():
        rest.start()

    @pl.when(owner == member)
    def _():
        pltpu.sync_copy(x_hbm.at[:, pl.ds(pl.multiple_of(offset, LANES), width)], xc_ref)

    for s in range(1, members):

        @pl.when(lax.rem(member - owner + members, members) == s)
        def _():
            pltpu.sync_copy(got_refs[s - 1], xc_ref)

    for c in early:
        c.wait()

    def write(target, z):
        high, low = split(z)

        def product(xt):
            return jnp.dot(xt, high, preferred_element_type=F32) + jnp.dot(
                xt, low, preferred_element_type=F32
            )

        @pl.when(member == 0)
        def _():
            target[width:, :] = product(xt_ref[width:, :])

        @pl.when(member > 0)
        def _():
            target[...] = product(xt_ref[...])

    def trailing(r):
        return pltpu.make_async_copy(out_ref.at[r, :, :width], trail_hbm.at[r], sent.at[r])

    def sides(j):
        at = pl.ds(pl.multiple_of(j * tile, LANES), tile)
        return pltpu.make_async_copy(
            out_ref.at[options + j], right_hbm.at[:, at], sent.at[options + j]
        )

    def system(r, _):
        target = out_ref.at[r, :, :width]

        @pl.when(vox == 0)
        def _():
            target[...] = jnp.zeros((rows, width), F32)

        @pl.when(vox > 0)
        def _():
            at = pl.ds(pl.multiple_of(r * 2 * time, LANES), 2 * time)
            xc = xc_ref[...]
            z = jnp.dot(ks_ref[:, at], jnp.concatenate([xc, xc], axis=0), preferred_element_type=F32)
            write(target, z * (1.0 / time))

            @pl.when(member == 0)
            def _():
                target[:width, :] = jnp.zeros((width, width), F32)

            @pl.when(owner == member)
            def _():
                to = pl.ds(pl.multiple_of(offset, LANES), width)
                ridge = jnp.zeros((1, width), F32)
                for g in range(groups):
                    ridge = jnp.where(label_ref[...] == g, weights_ref[r, g], ridge)
                row = lax.broadcasted_iota(jnp.int32, (width, width), 0)
                col = lax.broadcasted_iota(jnp.int32, (width, width), 1)
                target[to, :] += jnp.where(row == col, ridge, 0.0)

        trailing(r).start()
        return 0

    lax.fori_loop(0, options, system, 0)
    for c in late:
        c.wait()

    @pl.when(member == 0)
    def _():
        rest.wait()

    def signals(j, _):
        target = out_ref.at[options + j]
        start = j * tile
        lane = lax.broadcasted_iota(jnp.int32, (1, LANES), 1)
        chosen = []
        for c in range(tile // LANES):
            value = jnp.zeros((1, LANES), F32)
            for i in range(LANES // GROUP):
                choice = choice_ref[start // GROUP + c * (LANES // GROUP) + i].astype(F32)
                value = jnp.where(lane >= i * GROUP, choice, value)
            chosen.append(value)
        chosen = jnp.concatenate(chosen, axis=1)
        y = y_ref[:, pl.ds(pl.multiple_of(start, LANES), tile)].astype(F32)
        for r in range(options):
            masked = jnp.where(chosen == float(r), y, 0.0).astype(BF16)
            for h in range(2):
                to = (2 * r + h) * time
                ym_ref[to : to + time, :] = masked
        ym = ym_ref[...]
        write(target, jnp.dot(ks_ref[...], ym, preferred_element_type=F32) * time**-0.5)

        @pl.when(member == 0)
        def _():
            target[:width, :] = jnp.dot(ws_ref[...], ym, preferred_element_type=F32)

        sides(j).start()
        return 0

    lax.fori_loop(0, tiles - options, signals, 0)
    for r in range(options):
        trailing(r).wait()
    for j in range(tiles - options):
        sides(j).wait()


def apply(weights, choice, labels, x, xt, w, k, gots, ys):
    rows, time = xt.shape
    width = labels.shape[1]
    voxels = ys[0].shape[1]
    options = weights.shape[0]
    tile = min(512, voxels)
    tiles = options + voxels // tile
    stack = 2 * options * time
    smem = pl.BlockSpec(memory_space=pltpu.SMEM)
    vmem = pl.BlockSpec(memory_space=pltpu.VMEM)
    hbm = pl.BlockSpec(memory_space=pl.ANY)
    return pl.pallas_call(
        lambda *refs: apply_kernel(len(gots) + 1, *refs),
        out_shape=(
            jax.ShapeDtypeStruct((options, rows, width), F32),
            jax.ShapeDtypeStruct((rows, voxels), F32),
        ),
        in_specs=[smem, smem, vmem] + [hbm] * (4 + len(gots) + len(ys)),
        out_specs=(hbm, hbm),
        scratch_shapes=[
            pltpu.VMEM((rows, time), BF16),
            pltpu.VMEM((time, width), BF16),
            pltpu.VMEM((time, stack), BF16),
            pltpu.VMEM((width, stack), BF16),
            pltpu.VMEM((time, voxels), BF16),
            pltpu.VMEM((stack, tile), BF16),
            pltpu.VMEM((tiles, rows, max(tile, width)), F32),
            pltpu.SemaphoreType.DMA((3 + len(ys),)),
            pltpu.SemaphoreType.DMA((tiles,)),
        ],
        name="apply",
    )(weights, choice, labels, x, xt, w, k, *gots, *ys)


def local(
    design_matrix, measured_signals, predictor_group_label, shrinkage_weights, target_shrink_choice
):
    nt, nv, nf = (lax.axis_size(a) for a in AXES)
    members = nt * nf
    vox = lax.axis_index("vox")
    rows = design_matrix.shape[1]
    width = predictor_group_label.shape[0]

    def device(g, v):
        return (g // nf * nv + v) * nf + g % nf

    def share(block, owner):
        gots = []
        for s in range(1, members):
            pairs = [(device(owner(v), v), device((owner(v) + s) % members, v)) for v in range(nv)]
            gots.append(lax.ppermute(block, AXES, pairs))
        small = len(gots) * block.size * block.dtype.itemsize <= 2**20
        return [resident(got) for got in gots] if small else gots

    firsts = share(design_matrix[:, :width], lambda v: 0)
    labels = predictor_group_label[None, :]
    known = 1
    while known < nv:
        got = lax.ppermute(labels, "vox", [(a, a + known) for a in range(known)])
        known *= 2
        if known < nv:
            labels = jnp.where((vox >= known // 2) & (vox < known), got, labels)
    ys = [measured_signals]
    for s in range(1, nt):
        pairs = [(a, (a + s) % nt) for a in range(nt)]
        ys.append(resident(lax.ppermute(measured_signals, "tm", pairs)))
    source = vox * width // rows
    own = lax.dynamic_slice_in_dim(design_matrix, vox * width - source * rows, width, 1)
    columns = share(own, lambda v: v * width // rows)

    w, k, xt = factor(
        shrinkage_weights, design_matrix, resident(labels), resident(got), firsts
    )
    return apply(
        shrinkage_weights,
        target_shrink_choice,
        predictor_group_label[None, :],
        design_matrix,
        xt,
        w,
        k,
        columns,
        ys,
    )


def solution(mesh):
    return jax.shard_map(
        local,
        mesh=mesh,
        in_specs=(P(None, ("tm", "feat")), P("tm", "vox"), P("vox"), P(), P("vox")),
        out_specs=(P(None, ("tm", "feat"), "vox"), P(("tm", "feat"), "vox")),
        check_vma=False,
    )
```

```python
import jax
import jax.numpy as jnp
from jax import lax
from jax.experimental import pallas as pl
from jax.experimental.pallas import tpu as pltpu
from jax.sharding import PartitionSpec as P

GROUP = 64
F32 = jnp.float32
BF16 = jnp.bfloat16
FIRST = (((0,), (0,)), ((), ()))
LAST = (((1,), (1,)), ((), ()))
LANES = 128
B = 64
H = 16
AXES = ("tm", "vox", "feat")


def lane_b(v, index):
    return jnp.take_along_axis(v, index, axis=1, mode="promise_in_bounds")


def sub_b(v, row):
    return jnp.broadcast_to(v[row : row + 1, :], v.shape)


def inverse_factors(tile):
    n = B // H
    lanes = lax.broadcasted_iota(jnp.int32, (H, LANES), 1)
    subs = lax.broadcasted_iota(jnp.int32, (H, LANES), 0)
    base = jnp.where(lanes < B, 0, B)
    lane = lanes - base
    st = [tile[H * i : H * i + H, :] for i in range(n)]
    done = []
    for s in range(n):
        index = [base + (H * s + j) for j in range(H)]
        pivot = (lane >= H * s) & (lane < H * s + H)
        c = [lane_b(st[s], index[j]) for j in range(H)]
        row = jnp.where(pivot, jnp.where(lane - H * s == subs, 1.0, 0.0), st[s])
        out = row
        for j in range(H):
            d = sub_b(c[j], j)
            recip = 1.0 / d
            here = subs == j
            rb = sub_b(row, j)
            out = jnp.where(here, rb * lax.rsqrt(d), out)
            scaled = rb * recip
            row = jnp.where(here, scaled, row - c[j] * scaled)
            for l in range(j + 1, H):
                scaled = sub_b(c[l], j) * recip
                c[l] = jnp.where(here, scaled, c[l] - c[j] * scaled)
        done.append(jnp.where(lane < H * s + H, out, 0.0))
        if s + 1 < n:
            v = [sub_b(row, j) for j in range(H)]
            for t in range(s + 1, n):
                acc = jnp.where(pivot, 0.0, st[t])
                for j in range(H):
                    acc = acc - lane_b(st[t], index[j]) * v[j]
                st[t] = acc
    return jnp.concatenate(done, axis=0)


def split3(v):
    high = v.astype(BF16)
    rest = v - high.astype(F32)
    mid = rest.astype(BF16)
    return high, mid, (rest - mid.astype(F32)).astype(BF16)


def resident(v):
    return pltpu.with_memory_space_constraint(v, pltpu.VMEM)


def split(v):
    high = v.astype(BF16)
    return high, (v - high.astype(F32)).astype(BF16)


PRODUCTS = ((0, 0), (0, 1), (1, 0), (0, 2), (2, 0), (1, 1))


def stack(v, side, axis):
    parts = split3(v)
    return jnp.concatenate([parts[p[side]] for p in PRODUCTS], axis=axis)


def factor_kernel(weights_ref, own_ref, mine_ref, last_ref, *refs):
    firsts, refs = refs[:-11], refs[-11:]
    w_out, k_out, xt_out = refs[:3]
    ws_ref, ks_ref, k_ref, xt_ref, x_ref, label_ref, xo_ref, sems = refs[3:]
    member = lax.axis_index(("tm", "feat"))
    vox = lax.axis_index("vox")
    width = mine_ref.shape[1]

    @pl.when(member == 0)
    def _():
        x_ref[...] = own_ref[:, :width]

    for s in range(len(firsts)):

        @pl.when(member == s + 1)
        def _():
            pltpu.sync_copy(firsts[s], x_ref)

    received = 2 * vox >= lax.axis_size("vox")

    @pl.when(received)
    def _():
        pltpu.sync_copy(last_ref, label_ref)

    @pl.when(jnp.logical_not(received))
    def _():
        pltpu.sync_copy(mine_ref, label_ref)

    groups = weights_ref.shape[1]
    time = x_ref.shape[0]
    blocks = width // B
    copies = []

    def send(source, target):
        copies.append(pltpu.make_async_copy(source, target, sems.at[len(copies)]))
        copies[-1].start()

    iota = lambda d, shape: lax.broadcasted_iota(jnp.int32, shape, d)
    eye = jnp.where(iota(0, (time, time)) == iota(1, (time, time)), 1.0, 0.0)
    xt_ref[...] = lax.dot_general(
        x_ref[...], eye.astype(BF16), FIRST, preferred_element_type=F32
    ).astype(BF16)
    low = iota(1, (B, LANES)) < B
    diagonal = iota(1, (B, LANES)) - jnp.where(low, 0, B) == iota(0, (B, LANES))

    def rows(n):
        return slice(n * B, (n + 1) * B)

    def chunk(n):
        return slice(n // 2 * LANES, (n // 2 + 1) * LANES)

    def pair(first, second, n):
        move = 1 - n % 2
        both = [first, second]
        both[move] = pltpu.roll(both[move], B, 1)
        return both

    def ridge(n):
        label = jnp.broadcast_to(label_ref[:, chunk(n)], (8, LANES))
        both = []
        for r in range(2):
            value = jnp.zeros((8, LANES), F32)
            for g in range(groups):
                value = jnp.where(label == g, weights_ref[r, g], value)
            both.append(value)
        both = pair(*both, n)
        return jnp.where(diagonal, jnp.where(low, both[0][:1], both[1][:1]), 0.0)

    def thrice(left, right):
        parts = [jnp.dot(left, p, preferred_element_type=F32) for p in split3(right)]
        return parts[0] + (parts[1] + parts[2])

    def packed(n, q):
        xt = xt_ref[rows(n), :]
        total = 0.0
        parts = [split3(v) for v in q]
        for i in (2, 1, 0):
            right = jnp.concatenate([p[i] for p in parts], axis=0)
            total = total + lax.dot_general(xt, right, LAST, preferred_element_type=F32)
        return total * (1.0 / time)

    def schur(n, q):
        return packed(n, q) + ridge(n)

    def coupling(n, q):
        back = packed(n, q)
        xt = xt_ref[rows(n), :]
        empty = jnp.zeros((B, time), BF16)
        ahead = []
        for r in range(2):
            right = jnp.concatenate([xt, empty] if r == 0 else [empty, xt], axis=0)
            parts = jnp.concatenate(split3(q[r]), axis=0)
            v = lax.dot_general(parts, right, LAST, preferred_element_type=F32) * (1.0 / time)
            ahead.append(v[:B] + (v[B : 2 * B] + v[2 * B :]))
        turned = jnp.concatenate([jnp.where(low, back, 0.0), jnp.where(low, 0.0, back)], axis=0)
        return jnp.concatenate(ahead, axis=0), turned

    zeros = jnp.zeros((B, time), F32)
    q = [xt_ref[rows(0), :].astype(F32)] * 2
    tile = schur(0, q)
    across, turned = coupling(1, q)
    ahead = schur(1, [xt_ref[rows(1), :].astype(F32)] * 2)
    for n in range(blocks):
        inverse = inverse_factors(tile)
        inv = stack(inverse, 0, 1)
        if n + 1 < blocks:
            p = jnp.dot(inv, stack(across, 1, 0), preferred_element_type=F32)
            pt = lax.dot_general(
                stack(turned, 0, 1), stack(inverse, 1, 1), LAST, preferred_element_type=F32
            )
            left, right = split3(pt), split3(p)
            pp = sum(
                jnp.dot(left[i], right[j], preferred_element_type=F32) for i, j in PRODUCTS[::-1]
            )
            tile = ahead - jnp.where(low, pp[:B], pp[B:])
        for r in range(2):
            rhs = jnp.concatenate([q[0], zeros] if r == 0 else [zeros, q[1]], axis=0)
            w = jnp.dot(inv, stack(rhs, 1, 0), preferred_element_type=F32) * time**-0.5
            at = 2 * r * time
            ws_ref[rows(n), at : at + time], ws_ref[rows(n), at + time : at + 2 * time] = split(w)
            ww = lax.dot_general(stack(w, 0, 0), stack(w, 1, 0), FIRST, preferred_element_type=F32)
            k_ref[r] = (eye if n == 0 else k_ref[r]) - ww
        if n == 0:
            xo_ref[...] = lax.dot_general(
                own_ref[...], eye.astype(BF16), FIRST, preferred_element_type=F32
            ).astype(BF16)
        if n + 1 < blocks:
            last = n + 2 >= blocks
            xt = xt_ref[(n + 1) * B : (n + (2 if last else 3)) * B, :]
            qq = [thrice(xt, k_ref[r]) for r in range(2)]
            q = [v[:B] for v in qq]
            if not last:
                across, turned = coupling(n + 2, q)
                ahead = schur(n + 2, [v[B:] for v in qq])
    for r in range(2):
        at = 2 * r * time
        ks_ref[:, at : at + time], ks_ref[:, at + time : at + 2 * time] = split(k_ref[r])
    send(ks_ref, k_out)
    send(xo_ref, xt_out)

    @pl.when(member == 0)
    def _():
        pltpu.sync_copy(ws_ref, w_out)

    for c in copies:
        c.wait()


def factor(weights, x, labels, last, firsts):
    time, rows = x.shape
    width = labels.shape[1]
    stack = 2 * weights.shape[0] * time
    vmem = pl.BlockSpec(memory_space=pltpu.VMEM)
    hbm = pl.BlockSpec(memory_space=pl.ANY)
    return pl.pallas_call(
        factor_kernel,
        out_shape=(
            jax.ShapeDtypeStruct((width, stack), BF16),
            jax.ShapeDtypeStruct((time, stack), BF16),
            jax.ShapeDtypeStruct((rows, time), BF16),
        ),
        in_specs=[pl.BlockSpec(memory_space=pltpu.SMEM), vmem, hbm, hbm] + [hbm] * len(firsts),
        out_specs=(hbm, hbm, hbm),
        scratch_shapes=[
            pltpu.VMEM((width, stack), BF16),
            pltpu.VMEM((time, stack), BF16),
            pltpu.VMEM((2, time, time), F32),
            pltpu.VMEM((width, time), BF16),
            pltpu.VMEM((time, width), BF16),
            pltpu.VMEM((1, width), jnp.int32),
            pltpu.VMEM((rows, time), BF16),
            pltpu.SemaphoreType.DMA((2,)),
        ],
        name="factor",
    )(weights, x, labels, last, *firsts)


def apply_kernel(members, weights_ref, choice_ref, label_ref, x_hbm, xt_hbm, w_hbm, k_hbm, *refs):
    got_refs, y_hbms = refs[: members - 1], refs[members - 1 : -11]
    trail_hbm, right_hbm = refs[-11:-9]
    xt_ref, xc_ref, ks_ref, ws_ref, y_ref, ym_ref, out_ref, sems, sent = refs[-9:]
    options, groups = weights_ref.shape
    tiles, rows, tile = out_ref.shape
    time, width = xc_ref.shape
    n = len(y_hbms)
    part = time // n
    member = lax.axis_index(("tm", "feat"))
    vox = lax.axis_index("vox")
    tm = lax.axis_index("tm")
    owner = vox * width // rows
    offset = vox * width - owner * rows

    early = [
        pltpu.make_async_copy(k_hbm, ks_ref, sems.at[0]),
        pltpu.make_async_copy(xt_hbm, xt_ref, sems.at[1]),
    ]
    late = [
        pltpu.make_async_copy(
            y_hbms[s],
            y_ref.at[pl.ds(pl.multiple_of(lax.rem(tm - s + n, n) * part, part), part), :],
            sems.at[2 + s],
        )
        for s in range(n)
    ]
    rest = pltpu.make_async_copy(w_hbm, ws_ref, sems.at[2 + n])
    for c in early + late:
        c.start()

    @pl.when(member == 0)
    def _():
        rest.start()

    @pl.when(owner == member)
    def _():
        pltpu.sync_copy(x_hbm.at[:, pl.ds(pl.multiple_of(offset, LANES), width)], xc_ref)

    for s in range(1, members):

        @pl.when((vox > 0) & (lax.rem(member - owner + members, members) == s))
        def _():
            pltpu.sync_copy(got_refs[s - 1], xc_ref)

    for c in early:
        c.wait()

    def write(target, z):
        high, low = split(z)

        def product(xt):
            return jnp.dot(xt, high, preferred_element_type=F32) + jnp.dot(
                xt, low, preferred_element_type=F32
            )

        @pl.when(member == 0)
        def _():
            target[width:, :] = product(xt_ref[width:, :])

        @pl.when(member > 0)
        def _():
            target[...] = product(xt_ref[...])

    def trailing(r):
        return pltpu.make_async_copy(out_ref.at[r, :, :width], trail_hbm.at[r], sent.at[r])

    def sides(j):
        at = pl.ds(pl.multiple_of(j * tile, LANES), tile)
        return pltpu.make_async_copy(
            out_ref.at[options + j], right_hbm.at[:, at], sent.at[options + j]
        )

    def system(r, _):
        target = out_ref.at[r, :, :width]

        @pl.when(vox == 0)
        def _():
            target[...] = jnp.zeros((rows, width), F32)

        @pl.when(vox > 0)
        def _():
            at = pl.ds(pl.multiple_of(r * 2 * time, LANES), 2 * time)
            xc = xc_ref[...]
            z = jnp.dot(ks_ref[:, at], jnp.concatenate([xc, xc], axis=0), preferred_element_type=F32)
            write(target, z * (1.0 / time))

            @pl.when(member == 0)
            def _():
                target[:width, :] = jnp.zeros((width, width), F32)

            @pl.when(owner == member)
            def _():
                to = pl.ds(pl.multiple_of(offset, LANES), width)
                ridge = jnp.zeros((1, width), F32)
                for g in range(groups):
                    ridge = jnp.where(label_ref[...] == g, weights_ref[r, g], ridge)
                row = lax.broadcasted_iota(jnp.int32, (width, width), 0)
                col = lax.broadcasted_iota(jnp.int32, (width, width), 1)
                target[to, :] += jnp.where(row == col, ridge, 0.0)

        trailing(r).start()
        return 0

    lax.fori_loop(0, options, system, 0)
    for c in late:
        c.wait()

    @pl.when(member == 0)
    def _():
        rest.wait()

    def signals(j, _):
        target = out_ref.at[options + j]
        start = j * tile
        lane = lax.broadcasted_iota(jnp.int32, (1, LANES), 1)
        chosen = []
        for c in range(tile // LANES):
            value = jnp.zeros((1, LANES), F32)
            for i in range(LANES // GROUP):
                choice = choice_ref[start // GROUP + c * (LANES // GROUP) + i].astype(F32)
                value = jnp.where(lane >= i * GROUP, choice, value)
            chosen.append(value)
        chosen = jnp.concatenate(chosen, axis=1)
        y = y_ref[:, pl.ds(pl.multiple_of(start, LANES), tile)].astype(F32)
        for r in range(options):
            masked = jnp.where(chosen == float(r), y, 0.0).astype(BF16)
            for h in range(2):
                to = (2 * r + h) * time
                ym_ref[to : to + time, :] = masked
        ym = ym_ref[...]
        write(target, jnp.dot(ks_ref[...], ym, preferred_element_type=F32) * time**-0.5)

        @pl.when(member == 0)
        def _():
            target[:width, :] = jnp.dot(ws_ref[...], ym, preferred_element_type=F32)

        sides(j).start()
        return 0

    lax.fori_loop(0, tiles - options, signals, 0)
    for r in range(options):
        trailing(r).wait()
    for j in range(tiles - options):
        sides(j).wait()


def apply(weights, choice, labels, x, xt, w, k, gots, ys):
    rows, time = xt.shape
    width = labels.shape[1]
    voxels = ys[0].shape[1]
    options = weights.shape[0]
    tile = min(512, voxels)
    tiles = options + voxels // tile
    stack = 2 * options * time
    smem = pl.BlockSpec(memory_space=pltpu.SMEM)
    vmem = pl.BlockSpec(memory_space=pltpu.VMEM)
    hbm = pl.BlockSpec(memory_space=pl.ANY)
    return pl.pallas_call(
        lambda *refs: apply_kernel(len(gots) + 1, *refs),
        out_shape=(
            jax.ShapeDtypeStruct((options, rows, width), F32),
            jax.ShapeDtypeStruct((rows, voxels), F32),
        ),
        in_specs=[smem, smem, vmem] + [hbm] * (4 + len(gots) + len(ys)),
        out_specs=(hbm, hbm),
        scratch_shapes=[
            pltpu.VMEM((rows, time), BF16),
            pltpu.VMEM((time, width), BF16),
            pltpu.VMEM((time, stack), BF16),
            pltpu.VMEM((width, stack), BF16),
            pltpu.VMEM((time, voxels), BF16),
            pltpu.VMEM((stack, tile), BF16),
            pltpu.VMEM((tiles, rows, max(tile, width)), F32),
            pltpu.SemaphoreType.DMA((3 + len(ys),)),
            pltpu.SemaphoreType.DMA((tiles,)),
        ],
        name="apply",
    )(weights, choice, labels, x, xt, w, k, *gots, *ys)


def local(
    design_matrix, measured_signals, predictor_group_label, shrinkage_weights, target_shrink_choice
):
    nt, nv, nf = (lax.axis_size(a) for a in AXES)
    members = nt * nf
    vox = lax.axis_index("vox")
    rows = design_matrix.shape[1]
    width = predictor_group_label.shape[0]

    def device(g, v):
        return (g // nf * nv + v) * nf + g % nf

    def share(block, owner, takers):
        gots = []
        for s in range(1, members):
            pairs = [(device(owner(v), v), device((owner(v) + s) % members, v)) for v in takers]
            gots.append(lax.ppermute(block, AXES, pairs))
        small = len(gots) * block.size * block.dtype.itemsize <= 2**20
        return [resident(got) for got in gots] if small else gots

    firsts = share(design_matrix[:, :width], lambda v: 0, range(nv))
    labels = predictor_group_label[None, :]
    known = 1
    while known < nv:
        got = lax.ppermute(labels, "vox", [(a, a + known) for a in range(known)])
        known *= 2
        if known < nv:
            labels = jnp.where((vox >= known // 2) & (vox < known), got, labels)
    ys = [measured_signals]
    for s in range(1, nt):
        pairs = [(a, (a + s) % nt) for a in range(nt)]
        ys.append(resident(lax.ppermute(measured_signals, "tm", pairs)))
    source = vox * width // rows
    own = lax.dynamic_slice_in_dim(design_matrix, vox * width - source * rows, width, 1)
    columns = share(own, lambda v: v * width // rows, range(1, nv))

    w, k, xt = factor(
        shrinkage_weights, design_matrix, resident(labels), resident(got), firsts
    )
    return apply(
        shrinkage_weights,
        target_shrink_choice,
        predictor_group_label[None, :],
        design_matrix,
        xt,
        w,
        k,
        columns,
        ys,
    )


def solution(mesh):
    return jax.shard_map(
        local,
        mesh=mesh,
        in_specs=(P(None, ("tm", "feat")), P("tm", "vox"), P("vox"), P(), P("vox")),
        out_specs=(P(None, ("tm", "feat"), "vox"), P(("tm", "feat"), "vox")),
        check_vma=False,
    )
```
